32 devices in a mesh: row: 8 (over y, x, core), col: 4 (over z).
Axes of the slice: x: 2, y: 2, z: 4, core: 2. Of those that a mesh axis runs over, the one named last changes fastest.
Arguments:
- matrix: float32 [8, 3, 256, 4, 6, 256], P('row', None, None, 'col'), as said below
- checksum: float32 [8, 3, 256, 6, 256], P('row'), as said below
- failed: int32 [4], P('col'), may hold values from 0 to 3, as said below
Outputs:
- factored: float32 [8, 3, 256, 4, 6, 256], P('row', None, None, 'col')
- updated_checksum_result: float32 [8, 3, 256, 6, 256], P('row')
The draws below stay inside these ranges and needn't reach their ends.
Inputs may be any that keep to these rules, and one draw needn't show every extreme that they name: `failed`: a permutation of the grid column indices; entry 0 names the grid column whose tiles in matrix carry no information. With the lost grid column rebuilt from checksum, matrix is symmetric positive definite. `checksum`: for each grid row, the sum over all grid columns of the intact matrix's tiles, the lost column included.
All inputs are finite; a program needn't handle non-finite values.
Results may differ from the reference program's by a relative error of at most 0.0003.
Values sent between devices are 32-bit elements; how exact they have to be, the bound alone decides.
A program may use at most 128 MiB of HBM per device.

```python
import math
import jax
import jax.numpy as jnp
from jax import lax

B = 256
PANELS = 3
GRID_ROWS = 8
GRID_COLS = 4
NT = 24
TR = 3
TC = 6
ORDER = 6144


def intact_tiles(key):
    full_order = NT * B
    inner_width = 2 * B
    loadings = jax.random.normal(jax.random.fold_in(key, 5), (full_order, inner_width), jnp.float32)
    loadings = loadings / math.sqrt(inner_width)
    square = 2.0 * jnp.dot(loadings, loadings.T, precision=lax.Precision.HIGHEST)
    diagonal_lift = jax.random.uniform(jax.random.fold_in(key, 6), (full_order,), jnp.float32, 0.5, 1.5)
    square = square + jnp.diag(diagonal_lift)
    return square.reshape(TR, GRID_ROWS, B, TC, GRID_COLS, B).transpose(1, 0, 2, 4, 3, 5)


def column_order(key):
    return jax.random.permutation(jax.random.fold_in(key, 4517), jnp.arange(GRID_COLS, dtype=jnp.int32))


def draw_failed(key, part):
    return column_order(key)


def draw_matrix(key, part):
    blocks = intact_tiles(key)
    garbage = jax.random.normal(jax.random.fold_in(key, 7), blocks.shape, jnp.float32)
    column_ids = jnp.arange(GRID_COLS, dtype=jnp.int32).reshape(1, 1, 1, GRID_COLS, 1, 1)
    return jnp.where(column_ids == column_order(key)[0], garbage, blocks)


def draw_checksum(key, part):
    return jnp.sum(intact_tiles(key), axis=3)


def setup_inputs(seed: int = 0) -> dict:
    streams_of = jax.random.split(jax.random.key(seed), 4)
    return {
        "matrix": draw_matrix(jax.random.fold_in(streams_of[3], 71), 0),
        "checksum": draw_checksum(jax.random.fold_in(streams_of[3], 71), 0),
        "failed": draw_failed(jax.random.fold_in(streams_of[3], 71), 0),
    }


def to_natural(blocks):
    return blocks.transpose(1, 0, 2, 4, 3, 5).reshape(ORDER, ORDER)

def split_into_tiles(square):
    return square.reshape(TR, GRID_ROWS, B, TC, GRID_COLS, B).transpose(1, 0, 2, 4, 3, 5)

def reference(matrix, checksum, failed):
    missing_tiles = failed[0]
    column_ids = jnp.arange(GRID_COLS, dtype=jnp.int32).reshape(1, 1, 1, GRID_COLS, 1, 1)
    remaining_peers = jnp.sum(jnp.where(column_ids != missing_tiles, matrix, 0.0), axis=3)
    restored_tiles = jnp.where(column_ids == missing_tiles, (checksum - remaining_peers)[:, :, :, None], matrix)
    work = to_natural(restored_tiles)
    columns = []
    for panel in range(PANELS):
        start = panel * B
        factor = jnp.linalg.cholesky(work[start:start + B, start:start + B])
        below = work[start + B:, start:start + B]
        solved = jax.scipy.linalg.solve_triangular(factor, below.T, lower=True).T
        upper_zero = jnp.zeros((start, B), work.dtype)
        block_column = jnp.concatenate([upper_zero, factor, solved], axis=0)
        work = work - jnp.dot(block_column, block_column.T, precision=lax.Precision.HIGHEST)
        columns.append(block_column)
    tiles = split_into_tiles(work)
    updated_checksum_result = jnp.sum(tiles, axis=3)
    for panel in range(PANELS):
        panel_tiles = columns[panel].reshape(TR, GRID_ROWS, B, B).transpose(1, 0, 2, 3)
        tiles = tiles.at[:, :, :, panel % GRID_COLS, panel // GRID_COLS, :].set(panel_tiles)
    tile_rows = jnp.arange(GRID_ROWS)[:, None] + jnp.arange(TR)[None, :] * GRID_ROWS
    tile_cols = jnp.arange(GRID_COLS)[:, None] + jnp.arange(TC)[None, :] * GRID_COLS
    keep = tile_rows.reshape(GRID_ROWS, TR, 1, 1, 1, 1) >= tile_cols.reshape(1, 1, 1, GRID_COLS, TC, 1)
    factored = jnp.where(keep, tiles, 0.0)
    return (factored, updated_checksum_result)
```

```python
import jax
import jax.numpy as jnp
from jax import lax
from jax.sharding import PartitionSpec as P

PANELS = 3
EXACT = lax.Precision.HIGHEST
FAST = lax.Precision.HIGH


def dot_t(a, b, precision=EXACT):
    return lax.dot_general(a, b, (((1,), (1,)), ((), ())), precision=precision)


def dot(a, b, precision=EXACT):
    return lax.dot_general(a, b, (((1,), (0,)), ((), ())), precision=precision)


def shards(matrix, checksum, failed):
    rows_count = lax.axis_size("row")
    cols_count = lax.axis_size("col")
    row_index = lax.axis_index("row")
    column_position = lax.axis_index("col")
    tile_rows, width, tile_cols = (matrix.shape[1], matrix.shape[2], matrix.shape[4])
    own = matrix.reshape(tile_rows, width, tile_cols, width).transpose(0, 2, 1, 3)
    totals = checksum.reshape(tile_rows, width, tile_cols, width).transpose(0, 2, 1, 3)
    row_tiles = row_index + jnp.arange(tile_rows, dtype=jnp.int32) * rows_count
    col_tiles = column_position + jnp.arange(tile_cols, dtype=jnp.int32) * cols_count
    slots = (PANELS - 1) // cols_count + 1
    top_slots = (PANELS - 1) // rows_count + 1

    lost_column = lax.all_gather(failed, "col", axis=0, tiled=True)[0]
    lost = column_position == lost_column

    gathered = lax.all_gather(own[:, :slots], "col", axis=0)
    ids = jnp.arange(cols_count, dtype=jnp.int32).reshape(-1, 1, 1, 1, 1)
    others = jnp.sum(jnp.where(ids != lost_column, gathered, 0.0), axis=0)
    patch = totals[:, :slots] - others
    panels = []
    for k in range(PANELS):
        slot = k // cols_count
        panels.append(
            jnp.where(lost_column == k % cols_count, patch[:, slot], gathered[k % cols_count, :, slot])
        )

    lead = jnp.stack(
        [
            jnp.where(
                row_index == i % rows_count,
                jnp.stack([panels[k][i // rows_count] for k in range(i + 1)] + [
                    jnp.zeros((width, width), jnp.float32) for _ in range(i + 1, PANELS)
                ]),
                0.0,
            )
            for i in range(PANELS)
        ]
    )
    lead = lax.psum(lead, "row")

    need = [
        tile_cols
        if a < top_slots
        else min(tile_cols, (rows_count * (a + 1) - 1) // cols_count + 1)
        for a in range(tile_rows)
    ]
    packed = jnp.concatenate([own[a, : need[a]] for a in range(tile_rows)], axis=0)
    lead_done, packed = lax.optimization_barrier((lead, packed))
    lead = lead_done
    summed = lax.psum(jnp.where(lost, 0.0, packed), "col")
    filled = []
    start = 0
    for a in range(tile_rows):
        pad = jnp.zeros((tile_cols - need[a], width, width), jnp.float32)
        filled.append(jnp.concatenate([summed[start : start + need[a]], pad], axis=0))
        start += need[a]
    work = jnp.where(lost, totals - jnp.stack(filled), own)

    tops = jnp.stack(
        [
            jnp.where(
                row_index == i % rows_count,
                jnp.concatenate([work[i // rows_count], totals[i // rows_count]], axis=0),
                0.0,
            )
            for i in range(PANELS)
        ]
    )
    tops = lax.psum(tops, "row")

    identity = jnp.eye(width, dtype=jnp.float32)
    factor = {}
    inverse = []
    for k in range(PANELS):
        for i in range(k, PANELS):
            tile = lead[i, k]
            for m in range(k):
                tile = tile - dot_t(factor[i, m], factor[k, m])
            if i == k:
                factor[k, k] = jnp.linalg.cholesky(tile)
                inverse.append(
                    jax.scipy.linalg.solve_triangular(factor[k, k], identity, lower=True)
                )
            else:
                factor[i, k] = dot_t(tile, inverse[k])

    solved_rows = []
    for k in range(PANELS):
        block = panels[k].reshape(tile_rows * width, width)
        for m in range(k):
            block = block - dot_t(solved_rows[m], factor[k, m])
        block = dot_t(block, inverse[k]).reshape(tile_rows, width, width)
        block = jnp.where((row_tiles > k)[:, None, None], block, 0.0)
        block = jnp.where((row_tiles == k)[:, None, None], factor[k, k][None], block)
        solved_rows.append(block.reshape(tile_rows * width, width))

    flat = tops.transpose(0, 2, 1, 3).reshape(PANELS, width, 2 * tile_cols * width)
    solved_cols = []
    for k in range(PANELS):
        block = flat[k]
        for m in range(k):
            block = block - dot(factor[k, m], solved_cols[m])
        solved_cols.append(dot(inverse[k], block))

    rows_factor = jnp.concatenate(solved_rows, axis=1)
    cols_factor = jnp.concatenate(solved_cols, axis=0)
    split = tile_cols * width
    shape = (tile_rows, width, tile_cols, width)
    update = dot(rows_factor, cols_factor[:, :split], FAST).reshape(shape).transpose(0, 2, 1, 3)
    drop = dot(rows_factor, cols_factor[:, split:], FAST).reshape(shape).transpose(0, 2, 1, 3)
    new_totals = (totals - drop).transpose(0, 2, 1, 3)

    work = work - update
    front = []
    for b in range(slots):
        tiles = work[:, b]
        for k in range(PANELS):
            if k // cols_count == b:
                mine = solved_rows[k].reshape(tile_rows, width, width)
                tiles = jnp.where(column_position == k % cols_count, mine, tiles)
        front.append(tiles)
    work = jnp.concatenate([jnp.stack(front, axis=1), work[:, slots:]], axis=1)
    keep = (row_tiles[:, None] >= col_tiles[None, :])[:, :, None, None]
    factored = jnp.where(keep, work, 0.0).transpose(0, 2, 1, 3)
    return (factored.reshape(matrix.shape), new_totals.reshape(checksum.shape))


def solution(mesh):
    return jax.shard_map(
        shards,
        mesh=mesh,
        in_specs=(
            P("row", None, None, "col", None, None),
            P("row", None, None, None, None),
            P("col"),
        ),
        out_specs=(P("row", None, None, "col", None, None), P("row", None, None, None, None)),
        check_vma=False,
    )
```

```python
import jax
import jax.numpy as jnp
from jax import lax
from jax.sharding import PartitionSpec as P

PANELS = 3
EXACT = lax.Precision.HIGHEST
FAST = lax.Precision.HIGH


def dot_t(a, b, precision=EXACT):
    return lax.dot_general(a, b, (((1,), (1,)), ((), ())), precision=precision)


def dot(a, b, precision=EXACT):
    return lax.dot_general(a, b, (((1,), (0,)), ((), ())), precision=precision)


def factor_tile(tile):
    half = tile.shape[0] // 2
    identity = jnp.eye(half, dtype=jnp.float32)

    def base(block):
        lower = jnp.linalg.cholesky(block)
        return lower, jax.scipy.linalg.solve_triangular(lower, identity, lower=True)

    first, first_inv = base(tile[:half, :half])
    below = dot_t(tile[half:, :half], first_inv)
    second, second_inv = base(tile[half:, half:] - dot_t(below, below))
    below_inv = -dot(second_inv, dot(below, first_inv))
    zero = jnp.zeros((half, half), jnp.float32)
    return jnp.block([[first, zero], [below, second]]), jnp.block(
        [[first_inv, zero], [below_inv, second_inv]]
    )


def shards(matrix, checksum, failed):
    rows_count = lax.axis_size("row")
    cols_count = lax.axis_size("col")
    row_index = lax.axis_index("row")
    column_position = lax.axis_index("col")
    tile_rows, width, tile_cols = (matrix.shape[1], matrix.shape[2], matrix.shape[4])
    own = matrix.reshape(tile_rows, width, tile_cols, width).transpose(0, 2, 1, 3)
    totals = checksum.reshape(tile_rows, width, tile_cols, width).transpose(0, 2, 1, 3)
    row_tiles = row_index + jnp.arange(tile_rows, dtype=jnp.int32) * rows_count
    col_tiles = column_position + jnp.arange(tile_cols, dtype=jnp.int32) * cols_count
    slots = (PANELS - 1) // cols_count + 1
    top_slots = (PANELS - 1) // rows_count + 1

    lost_column = lax.all_gather(failed, "col", axis=0, tiled=True)[0]
    lost = column_position == lost_column

    pieces = []
    pairs = [(i, k) for i in range(PANELS) for k in range(i + 1)]
    for i, k in pairs:
        a, b, root = i // rows_count, k // cols_count, k % cols_count
        rebuilt = jnp.where(lost, totals[a, b], -own[a, b])
        plain = jnp.where(column_position == root, own[a, b], 0.0)
        piece = jnp.where(lost_column == root, rebuilt, plain)
        pieces.append(jnp.where(row_index == i % rows_count, piece, 0.0))
    lead = lax.psum(jnp.stack(pieces), ("row", "col"))

    need = [
        min(tile_cols, (rows_count * (a + 1) - 1) // cols_count + 1) for a in range(tile_rows)
    ]
    healthy = jnp.where(lost, 0.0, own)
    top_part = healthy[:top_slots, slots:]
    rest_part = jnp.concatenate(
        [healthy[a, slots : need[a]] for a in range(top_slots, tile_rows)], axis=0
    )
    front_part = own[:, :slots]
    lead, top_part, rest_part, front_part = lax.optimization_barrier(
        (lead, top_part, rest_part, front_part)
    )
    lead = dict(zip(pairs, [lead[n] for n in range(len(pairs))]))

    gathered = lax.all_gather(front_part, "col", axis=0)
    ids = jnp.arange(cols_count, dtype=jnp.int32).reshape(-1, 1, 1, 1, 1)
    others = jnp.sum(jnp.where(ids != lost_column, gathered, 0.0), axis=0)
    patch = totals[:, :slots] - others
    panels = []
    for k in range(PANELS):
        slot = k // cols_count
        panels.append(
            jnp.where(lost_column == k % cols_count, patch[:, slot], gathered[k % cols_count, :, slot])
        )
    front_work = jnp.where(lost, patch, own[:, :slots])

    top_sum = lax.psum(top_part, "col")
    top_back = jnp.where(lost, totals[:top_slots, slots:] - top_sum, own[:top_slots, slots:])
    top_work = jnp.concatenate([front_work[:top_slots], top_back], axis=1)

    tops = jnp.stack(
        [
            jnp.where(
                row_index == i % rows_count,
                jnp.concatenate([top_work[i // rows_count], totals[i // rows_count]], axis=0),
                0.0,
            )
            for i in range(PANELS)
        ]
    )
    tops = lax.psum(tops, "row")
    tops, rest_part = lax.optimization_barrier((tops, rest_part))
    rest_sum = lax.psum(rest_part, "col")

    factor = {}
    inverse = []
    for k in range(PANELS):
        for i in range(k, PANELS):
            tile = lead[i, k]
            for m in range(k):
                tile = tile - dot_t(factor[i, m], factor[k, m])
            if i == k:
                factor[k, k], made = factor_tile(tile)
                inverse.append(made)
            else:
                factor[i, k] = dot_t(tile, inverse[k])

    solved_rows = []
    for k in range(PANELS):
        block = panels[k].reshape(tile_rows * width, width)
        for m in range(k):
            block = block - dot_t(solved_rows[m], factor[k, m])
        block = dot_t(block, inverse[k]).reshape(tile_rows, width, width)
        block = jnp.where((row_tiles > k)[:, None, None], block, 0.0)
        block = jnp.where((row_tiles == k)[:, None, None], factor[k, k][None], block)
        solved_rows.append(block.reshape(tile_rows * width, width))

    flat = tops.transpose(0, 2, 1, 3).reshape(PANELS, width, 2 * tile_cols * width)
    solved_cols = []
    for k in range(PANELS):
        block = flat[k]
        for m in range(k):
            block = block - dot(factor[k, m], solved_cols[m])
        solved_cols.append(dot(inverse[k], block))

    rows_factor = jnp.concatenate(solved_rows, axis=1)
    cols_factor = jnp.concatenate(solved_cols, axis=0)
    split = tile_cols * width
    shape = (tile_rows, width, tile_cols, width)
    update = dot(rows_factor, cols_factor[:, :split], FAST).reshape(shape).transpose(0, 2, 1, 3)
    drop = dot(rows_factor, cols_factor[:, split:], FAST).reshape(shape).transpose(0, 2, 1, 3)
    new_totals = (totals - drop).transpose(0, 2, 1, 3)

    filled = []
    start = 0
    for a in range(top_slots, tile_rows):
        count = need[a] - slots
        pad = jnp.zeros((tile_cols - need[a], width, width), jnp.float32)
        filled.append(jnp.concatenate([rest_sum[start : start + count], pad], axis=0))
        start += count
    rest_back = jnp.where(
        lost, totals[top_slots:, slots:] - jnp.stack(filled), own[top_slots:, slots:]
    )
    rest_work = jnp.concatenate([front_work[top_slots:], rest_back], axis=1)
    work = jnp.concatenate([top_work, rest_work], axis=0) - update
    front = []
    for b in range(slots):
        tiles = work[:, b]
        for k in range(PANELS):
            if k // cols_count == b:
                mine = solved_rows[k].reshape(tile_rows, width, width)
                tiles = jnp.where(column_position == k % cols_count, mine, tiles)
        front.append(tiles)
    work = jnp.concatenate([jnp.stack(front, axis=1), work[:, slots:]], axis=1)
    keep = (row_tiles[:, None] >= col_tiles[None, :])[:, :, None, None]
    factored = jnp.where(keep, work, 0.0).transpose(0, 2, 1, 3)
    return (factored.reshape(matrix.shape), new_totals.reshape(checksum.shape))


def solution(mesh):
    return jax.shard_map(
        shards,
        mesh=mesh,
        in_specs=(
            P("row", None, None, "col", None, None),
            P("row", None, None, None, None),
            P("col"),
        ),
        out_specs=(P("row", None, None, "col", None, None), P("row", None, None, None, None)),
        check_vma=False,
    )
```
